768 devices in a mesh: grp: 8 (over x, core), rep: 96 (over z, y).
Axes of the slice: x: 4, y: 8, z: 12, core: 2. Of those that a mesh axis runs over, the one named last changes fastest.
Arguments:
- blocks: bfloat16 [1536, 64, 4096], P(('grp', 'rep')), may hold values from 0 to 10
- coords: int32 [1536, 3], P(('grp', 'rep')), may hold values from 0 to 767, as said below
- factor_a: float32 [49152, 128], P(('grp', 'rep')), may hold values from 0 to 1
- factor_b: bfloat16 [8192, 128], P('grp'), may hold values from 0.049804688 to 1
- factor_c: bfloat16 [8192, 128], P('grp'), may hold values from 0.049804688 to 1
Outputs:
- updated_a: float32 [49152, 128], P(('grp', 'rep'))
The draws below stay inside these ranges and needn't reach their ends.
Inputs may be any that keep to these rules, and one draw needn't show every extreme that they name: Row n of coords holds first, second and third coordinates below 768, 128, 128. Among the 2 blocks of one device, for each mode, the values coordinate // 96 (first mode) or coordinate // 16 (second and third) take any one value at most 2 times.
All inputs are finite; a program needn't handle non-finite values.
Results may differ from the reference program's by a relative error of at most 0.00072.
Values may be sent and summed in bfloat16 or wider, within the bound.
A program may use at most 32 MiB of HBM per device.

```python
import math
import jax
import jax.numpy as jnp
from jax import lax

R = 128
BS = 64
NBLK = 2
JB_DEV = 16
CAP = 2
PART_BLK = 96
IBLK = 768
JBLK = 128
N_GRP = 8
DEVICES = 768


def draw_coords(key, part):

    def per_device(device):
        dev_key = jax.random.fold_in(key, device)
        columns = []
        for mode_idx, extent in ((0, PART_BLK), (1, JB_DEV), (2, JB_DEV)):
            order_pos = jax.random.permutation(jax.random.fold_in(dev_key, 3 * mode_idx), NBLK)
            owners_perm = jax.random.permutation(jax.random.fold_in(dev_key, 3 * mode_idx + 1), N_GRP)
            owner = owners_perm[order_pos // CAP]
            offset = jax.random.randint(jax.random.fold_in(dev_key, 3 * mode_idx + 2), (NBLK,), 0, extent)
            columns.append(owner * extent + offset)
        return jnp.stack(columns, 1)
    return jax.vmap(per_device)(jnp.arange(DEVICES)).reshape(-1, 3).astype(jnp.int32)


def block_levels(key, shape, cuts, least, largest):
    def one(position, blocks):
        draws = jax.random.uniform(jax.random.fold_in(jax.random.fold_in(key, 6), position), (blocks,), jnp.float32, least / len(cuts), largest / len(cuts))
        return jnp.repeat(jnp.exp(draws), shape[position] // blocks).reshape((-1,) + (1,) * (len(shape) - position - 1))

    factor_of = one(*cuts[0])
    for cut in cuts[1:]:
        factor_of = factor_of * one(*cut)
    return factor_of


def setup_inputs(seed: int = 0) -> dict:
    splits = jax.random.split(jax.random.key(seed), 6)
    blocks = jnp.clip(10.0 * jax.random.uniform(splits[0], (DEVICES * NBLK, BS, BS * BS), jnp.float32) ** block_levels(splits[0], (DEVICES * NBLK, BS, BS * BS), ((0, 768),), -0.2, 0.2), 0.0, 10.0).astype(jnp.bfloat16)
    coords = draw_coords(jax.random.fold_in(splits[5], 71), 0)
    factor_a = jnp.clip(1.0 * jax.random.uniform(splits[2], (IBLK * BS, R), jnp.float32) ** block_levels(splits[2], (IBLK * BS, R), ((0, 768),), -0.2, 0.2), 0.0, 1.0)
    factor_b = jnp.clip(jnp.exp(math.log(1.0) - 2.9996462 * jax.random.uniform(splits[3], (JBLK * BS, R), jnp.float32) ** block_levels(splits[3], (JBLK * BS, R), ((0, 8),), -0.2, 0.2)), 0.049804688, 1.0).astype(jnp.bfloat16)
    factor_c = jnp.clip(jnp.exp(math.log(1.0) - 2.9996462 * jax.random.uniform(splits[4], (JBLK * BS, R), jnp.float32) ** block_levels(splits[4], (JBLK * BS, R), ((0, 8),), -0.2, 0.2)), 0.049804688, 1.0).astype(jnp.bfloat16)
    return dict(blocks=blocks, coords=coords, factor_a=factor_a, factor_b=factor_b, factor_c=factor_c)


def reference(blocks, coords, factor_a, factor_b, factor_c):
    rows_b = factor_b.reshape(-1, BS, R)
    rows_c = factor_c.reshape(-1, BS, R)

    def per_block(pair):
        block_x, coord_row = pair
        left = rows_b[coord_row[1]].astype(jnp.float32)
        right = rows_c[coord_row[2]].astype(jnp.float32)
        khatri = (left[:, None, :] * right[None, :, :]).astype(jnp.bfloat16).reshape(BS * BS, R)
        return jnp.dot(block_x, khatri, preferred_element_type=jnp.float32)
    partial_rows = lax.map(per_block, (blocks, coords))
    mttkrp = jnp.zeros((IBLK, BS, R), jnp.float32).at[coords[:, 0]].add(partial_rows).reshape(IBLK * BS, R)
    dims = (((0,), (0,)), ((), ()))
    gram_b = lax.dot_general(factor_b, factor_b, dims, preferred_element_type=jnp.float32)
    gram_c = lax.dot_general(factor_c, factor_c, dims, preferred_element_type=jnp.float32)
    norm_b = jnp.sqrt(jnp.diagonal(gram_b))
    norm_c = jnp.sqrt(jnp.diagonal(gram_c))
    gram = gram_b / (norm_b[:, None] * norm_b[None, :]) * (gram_c / (norm_c[:, None] * norm_c[None, :]))
    target = mttkrp / (norm_b * norm_c)[None, :]

    def column_step(column, factor):
        g_column = lax.dynamic_slice_in_dim(gram, column, 1, 1)
        predicted = jnp.dot(factor, g_column, precision=lax.Precision.HIGHEST)
        m_column = lax.dynamic_slice_in_dim(target, column, 1, 1)
        a_column = lax.dynamic_slice_in_dim(factor, column, 1, 1)
        pivot = lax.dynamic_slice_in_dim(g_column, column, 1, 0)
        updated = jnp.maximum(a_column + (m_column - predicted) / pivot, 0.0)
        return lax.dynamic_update_slice_in_dim(factor, updated, column, 1)
    return lax.fori_loop(0, R, column_step, factor_a)
```

```python
import functools

import jax
import jax.numpy as jnp
from jax import lax
from jax.experimental import pallas as pl
from jax.experimental.pallas import tpu as pltpu
from jax.sharding import PartitionSpec as P

R = 128
BS = 64
CAP = 2
NC = 2
NY = 8
ROWS_Y = 32
MESH = pl.DeviceIdType.MESH


def slot_of(owner):
    count = owner.shape[0]
    same_peer = owner[:, None] == owner[None, :]
    earlier = jnp.arange(count)[None, :] < jnp.arange(count)[:, None]
    return jnp.sum(jnp.logical_and(same_peer, earlier), axis=1)


def gram_of(factor):
    dims = (((0,), (0,)), ((), ()))
    return lax.dot_general(factor, factor, dims, preferred_element_type=jnp.float32)


class Ring:
    def __init__(self, n, me, peer, region, land, send, recv, rows):
        self.n, self.me, self.peer = n, me, peer
        self.region, self.land = region, land
        self.send, self.recv = send, recv
        self.half = n // 2
        self.rows = rows
        self.live = {}

    def at(self, offset):
        return lax.rem(self.me + (offset + 2 * self.n), self.n)

    def span(self, way, step):
        low, high = self.rows
        middle = (low + high) // 2
        if step == 1:
            return (low, middle) if way == 0 else (middle, high)
        return low, high

    def start(self, step):
        for way in (0, 1):
            sign = 1 - 2 * way
            low, high = self.span(way, step)
            copy = pltpu.make_async_remote_copy(
                src_ref=self.region(self.at(sign * (self.half + 1 - step)), low, high),
                dst_ref=self.land(way, step - 1, low, high),
                send_sem=self.send.at[way, step - 1],
                recv_sem=self.recv.at[way, step - 1],
                device_id=self.peer(self.at(sign)),
                device_id_type=MESH,
            )
            copy.start()
            self.live[way, step] = copy

    def finish(self, step):
        for way in (0, 1):
            sign = 1 - 2 * way
            low, high = self.span(way, step)
            self.live[way, step].wait_recv()
            mine = self.region(self.at(sign * (self.half - step)), low, high)
            mine[...] = mine[...] + self.land(way, step - 1, low, high)[...]

    def drain(self):
        for copy in self.live.values():
            copy.wait_send()


def exchange_kernel(
    n_x, n_z, load_ref, gram_ref, out_ref, gsum_ref,
    held, dense, gbuf, land_y, land_x, land_x2, land_y2,
    zs, zr, cs, cr, gs, gr, ys, yr, xs, xr, x2s, x2r, y2s, y2r,
):
    grp, rep = lax.axis_index("grp"), lax.axis_index("rep")
    n_grp = n_x * NC
    my_x, my_c = grp // NC, lax.rem(grp, NC)
    my_z, my_y = rep // NY, lax.rem(rep, NY)
    half_z = n_z // 2

    def z_at(offset):
        return lax.rem(my_z + (offset + 2 * n_z), n_z)

    def z_peer(z):
        return {"grp": grp, "rep": z * NY + my_y}

    def y_peer(y):
        return {"grp": grp, "rep": my_z * NY + y}

    def x_peer(x):
        return {"grp": x * NC + my_c, "rep": rep}

    def grp_peer(g):
        return {"grp": g, "rep": rep}

    barrier = pltpu.get_barrier_semaphore()
    greeted = [z_peer(z_at(1)), z_peer(z_at(-1))]
    greeted += [y_peer(lax.rem(my_y + 1, NY)), y_peer(lax.rem(my_y + NY - 1, NY))]
    greeted += [grp_peer(lax.rem(grp + k, n_grp)) for k in range(1, n_grp)]
    for who in greeted:
        pl.semaphore_signal(barrier, inc=1, device_id=who, device_id_type=MESH)
    pl.semaphore_wait(barrier, len(greeted))

    def remote(src, dst, send, recv, who):
        copy = pltpu.make_async_remote_copy(
            src_ref=src, dst_ref=dst, send_sem=send, recv_sem=recv,
            device_id=who, device_id_type=MESH,
        )
        copy.start()
        return copy

    sent = []
    partner = grp_peer(my_x * NC + (1 - my_c))
    z_live, c_live = {}, {}

    def pass_on(step, way, piece):
        origin = z_at(-(step - 1) if way == 0 else step - 1)
        src = load_ref.at[piece] if step == 1 else held.at[origin, my_c, piece]
        copy = remote(
            src, held.at[origin, my_c, piece],
            zs.at[way, step - 1, piece], zr.at[way, step - 1, piece],
            z_peer(z_at(1 if way == 0 else -1)),
        )
        z_live[step, way, piece] = copy
        sent.append(copy)

    def hand_over(offset, piece):
        origin = z_at(offset)
        src = load_ref.at[piece] if offset == 0 else held.at[origin, my_c, piece]
        slot = offset + half_z
        copy = remote(
            src, held.at[origin, my_c, piece], cs.at[slot, piece], cr.at[slot, piece], partner
        )
        c_live[offset, piece] = copy
        sent.append(copy)

    for piece in range(2):
        for way in range(2):
            if 1 < half_z or piece == way:
                pass_on(1, way, piece)
    for piece in range(2):
        hand_over(0, piece)
    gram_live = []
    for k in range(1, n_grp):
        copy = remote(
            gram_ref, gbuf.at[grp], gs.at[k - 1], gr.at[k - 1],
            grp_peer(lax.rem(grp + k, n_grp)),
        )
        gram_live.append(copy)
        sent.append(copy)
    gbuf[grp] = gram_ref[...]
    for piece in range(2):
        held[my_z, my_c, piece] = load_ref[piece]

    def absorb(offset, first):
        origin = z_at(offset)
        marks = [held[origin, c, b, BS : BS + 8, :] for c in range(NC) for b in range(2)]
        for part in range(2):
            rows = slice(part * (BS // 2), (part + 1) * (BS // 2))
            parts = [held[origin, c, b, rows, :] for c in range(NC) for b in range(2)]

            def place(slot, carry):
                x, y = slot // NY, lax.rem(slot, NY)
                target = ((x * NC + my_c) * (n_z * NY) + my_z * NY + y).astype(jnp.float32)
                total = None if first else dense[x, y, rows, :]
                for mark, block in zip(marks, parts):
                    hit = jnp.concatenate([mark == target] * (BS // 16), axis=0)
                    term = jnp.where(hit, block, 0.0)
                    total = term if total is None else total + term
                dense[x, y, rows, :] = total
                return carry

            lax.fori_loop(0, n_x * NY, place, 0)

    def carried(step, way, piece):
        return step < half_z or piece == way

    waiting = [0]
    fresh = True
    for step in range(1, half_z + 1):
        arrived = []
        for offset in waiting:
            for piece in range(2):
                c_live[offset, piece].wait_recv()
            absorb(offset, fresh)
            fresh = False
        for piece in range(2):
            for way in range(2):
                if carried(step, way, piece):
                    z_live[step, way, piece].wait_recv()
                    if step < half_z and carried(step + 1, way, piece):
                        pass_on(step + 1, way, piece)
                    offset = -step if way == 0 else step
                    if step == half_z:
                        offset = -step
                    hand_over(offset, piece)
                    if offset not in arrived:
                        arrived.append(offset)
        waiting = arrived
    for offset in waiting:
        for piece in range(2):
            c_live[offset, piece].wait_recv()
        absorb(offset, fresh)

    y_first = Ring(
        NY, my_y, y_peer,
        lambda y, low, high: dense.at[:, y, low:high, :],
        lambda way, step, low, high: land_y.at[way, step, :, low:high, :],
        ys, yr, (0, ROWS_Y),
    )
    x_first = Ring(
        n_x, my_x, x_peer,
        lambda x, low, high: dense.at[x, :, low:high, :],
        lambda way, step, low, high: land_x.at[way, step, :, low - ROWS_Y : high - ROWS_Y, :],
        xs, xr, (ROWS_Y, BS),
    )
    x_last = Ring(
        n_x, my_x, x_peer,
        lambda x, low, high: dense.at[x, my_y, low:high, :],
        lambda way, step, low, high: land_x2.at[way, step, low:high, :],
        x2s, x2r, (0, ROWS_Y),
    )
    y_last = Ring(
        NY, my_y, y_peer,
        lambda y, low, high: dense.at[my_x, y, low:high, :],
        lambda way, step, low, high: land_y2.at[way, step, low - ROWS_Y : high - ROWS_Y, :],
        y2s, y2r, (ROWS_Y, BS),
    )

    def stages(first, second):
        yield lambda: first.start(1)
        for step in range(1, first.half + 1):
            def turn(step=step):
                first.finish(step)
                if step < first.half:
                    first.start(step + 1)
                else:
                    second.start(1)
            yield turn
        for step in range(1, second.half + 1):
            def turn(step=step):
                second.finish(step)
                if step < second.half:
                    second.start(step + 1)
            yield turn

    chain_y, chain_x = list(stages(y_first, x_last)), list(stages(x_first, y_last))
    for index in range(max(len(chain_y), len(chain_x))):
        for chain in (chain_y, chain_x):
            if index < len(chain):
                chain[index]()
        if index == 0:
            for copy in gram_live:
                copy.wait_recv()
            gsum_ref[...] = functools.reduce(lambda a, b: a + b, [gbuf[g] for g in range(n_grp)])
    out_ref[...] = dense[my_x, my_y]
    for copy in sent:
        copy.wait_send()
    for ring in (y_first, x_first, x_last, y_last):
        ring.drain()


def exchange(load, gram, n_x, n_z):
    half_z, half_y, half_x = n_z // 2, NY // 2, n_x // 2
    vmem = pl.BlockSpec(memory_space=pltpu.VMEM)
    dma = pltpu.SemaphoreType.DMA
    rest = BS - ROWS_Y
    return pl.pallas_call(
        functools.partial(exchange_kernel, n_x, n_z),
        out_shape=(
            jax.ShapeDtypeStruct((BS, R), jnp.float32),
            jax.ShapeDtypeStruct((2 * R, R), jnp.float32),
        ),
        in_specs=[vmem, vmem],
        out_specs=(vmem, vmem),
        scratch_shapes=[
            pltpu.VMEM((n_z, NC, 2, BS + 8, R), jnp.float32),
            pltpu.VMEM((n_x, NY, BS, R), jnp.float32),
            pltpu.VMEM((n_x * NC, 2 * R, R), jnp.float32),
            pltpu.VMEM((2, half_y, n_x, ROWS_Y, R), jnp.float32),
            pltpu.VMEM((2, half_x, NY, rest, R), jnp.float32),
            pltpu.VMEM((2, half_x, ROWS_Y, R), jnp.float32),
            pltpu.VMEM((2, half_y, rest, R), jnp.float32),
            dma((2, half_z, 2)), dma((2, half_z, 2)),
            dma((n_z + 1, 2)), dma((n_z + 1, 2)),
            dma((n_x * NC - 1,)), dma((n_x * NC - 1,)),
            dma((2, half_y)), dma((2, half_y)),
            dma((2, half_x)), dma((2, half_x)),
            dma((2, half_x)), dma((2, half_x)),
            dma((2, half_y)), dma((2, half_y)),
        ],
        compiler_params=pltpu.CompilerParams(collective_id=0, has_side_effects=True),
        name="exchange",
    )(load, gram)


def sweep_kernel(m_ref, a_ref, g_ref, out_ref):
    gram_b, gram_c = g_ref[0:R, :], g_ref[R : 2 * R, :]
    down = lax.broadcasted_iota(jnp.int32, (R, R), 0)
    across = lax.broadcasted_iota(jnp.int32, (R, R), 1)
    on_diag = down == across

    def diagonals(square):
        kept = jnp.where(on_diag, square, 0.0)
        return jnp.sum(kept, axis=0, keepdims=True), jnp.sum(kept, axis=1, keepdims=True)

    b_row, b_col = diagonals(gram_b)
    c_row, c_col = diagonals(gram_c)
    b_row, b_col = jnp.sqrt(b_row), jnp.sqrt(b_col)
    c_row, c_col = jnp.sqrt(c_row), jnp.sqrt(c_col)
    gram = gram_b / (b_col * b_row) * (gram_c / (c_col * c_row))
    target = m_ref[...] / (b_row * c_row)
    pivot_row, pivot_col = diagonals(gram)
    later = jnp.where(down > across, gram, 0.0)
    known = jnp.dot(
        a_ref[...], later, precision=lax.Precision.HIGHEST, preferred_element_type=jnp.float32
    )
    start = ((target - known) / pivot_row).T
    weight = jnp.where(down > across, gram / pivot_col, 0.0)
    tiles = [start[8 * k : 8 * k + 8, :] for k in range(R // 8)]
    weights = [weight[8 * k : 8 * k + 8, :] for k in range(R // 8)]
    for r in range(R):
        own, sub = r // 8, r % 8
        fixed = jnp.maximum(jnp.broadcast_to(tiles[own][sub : sub + 1, :], (8, BS)), 0.0)
        for k in range(own, R // 8):
            if k == own and sub == 7:
                continue
            scale = jnp.broadcast_to(weights[k][:, r : r + 1], (8, BS))
            tiles[k] = tiles[k] - scale * fixed
    out_ref[...] = jnp.maximum(jnp.concatenate(tiles, axis=0), 0.0).T


def sweep(mttkrp, factor_a, gram):
    vmem = pl.BlockSpec(memory_space=pltpu.VMEM)
    return pl.pallas_call(
        sweep_kernel,
        out_shape=jax.ShapeDtypeStruct((BS, R), jnp.float32),
        in_specs=[vmem] * 3,
        out_specs=vmem,
        name="sweep",
    )(mttkrp, factor_a, gram)


def body(blocks, coords, factor_a, factor_b, factor_c):
    n_grp = lax.axis_size("grp")
    n_rep = lax.axis_size("rep")
    nblk_here = blocks.shape[0]
    jb_here = factor_b.shape[0] // BS
    first_row = coords[:, 0]
    second_row = coords[:, 1]
    third_row = coords[:, 2]
    peer_b = second_row // jb_here
    peer_c = third_row // jb_here
    slot_b = slot_of(peer_b)
    slot_c = slot_of(peer_c) + CAP
    wanted = jnp.zeros((n_grp, 2 * CAP), jnp.int32)
    wanted = wanted.at[peer_b, slot_b].set(second_row % jb_here)
    wanted = wanted.at[peer_c, slot_c].set(third_row % jb_here + jb_here)
    lookup_rows = jnp.concatenate([factor_b, factor_c], 0).reshape(2 * jb_here, BS, R)
    fetched = lax.all_to_all(
        lookup_rows[lax.all_to_all(wanted, "grp", split_axis=0, concat_axis=0, tiled=True)],
        "grp",
        split_axis=0,
        concat_axis=0,
        tiled=True,
    )
    left_rows = fetched[peer_b, slot_b]
    right_rows = fetched[peer_c, slot_c]
    gram_part = jnp.concatenate([gram_of(factor_b), gram_of(factor_c)], 0)
    khatri = (
        left_rows.astype(jnp.float32)[:, :, None, :] * right_rows.astype(jnp.float32)[:, None, :, :]
    )
    khatri = khatri.astype(jnp.bfloat16).reshape(nblk_here, BS * BS, R)
    partial_rows = jnp.einsum("bix,bxr->bir", blocks, khatri, preferred_element_type=jnp.float32)
    marks = jnp.broadcast_to(first_row.astype(jnp.float32)[:, None, None], (nblk_here, 8, R))
    load = jnp.concatenate([partial_rows, marks], 1)
    mttkrp, gram = exchange(load, gram_part, n_grp // NC, n_rep // NY)
    return sweep(mttkrp, factor_a, gram)


def solution(mesh):
    placed = (
        P(("grp", "rep"), None, None),
        P(("grp", "rep"), None),
        P(("grp", "rep"), None),
        P("grp", None),
        P("grp", None),
    )
    return jax.shard_map(
        body, mesh=mesh, in_specs=placed, out_specs=P(("grp", "rep"), None), check_vma=False
    )
```

```python
import functools

import jax
import jax.numpy as jnp
from jax import lax
from jax.experimental import pallas as pl
from jax.experimental.pallas import tpu as pltpu
from jax.sharding import PartitionSpec as P

R = 128
BS = 64
NC = 2
NY = 8
ROWS_Y = 24
MESH = pl.DeviceIdType.MESH


class Ring:
    def __init__(self, n, me, peer, region, land, send, recv, rows):
        self.n, self.me, self.peer = n, me, peer
        self.region, self.land = region, land
        self.send, self.recv = send, recv
        self.half = n // 2
        self.rows = rows
        self.live = {}

    def at(self, offset):
        return lax.rem(self.me + (offset + 2 * self.n), self.n)

    def span(self, way, step):
        low, high = self.rows
        middle = low + (high - low) // 16 * 8
        if step == 1:
            return (low, middle) if way == 0 else (middle, high)
        return low, high

    def start(self, step):
        for way in (0, 1):
            sign = 1 - 2 * way
            low, high = self.span(way, step)
            copy = pltpu.make_async_remote_copy(
                src_ref=self.region(self.at(sign * (self.half + 1 - step)), low, high),
                dst_ref=self.land(way, step - 1, low, high),
                send_sem=self.send.at[way, step - 1],
                recv_sem=self.recv.at[way, step - 1],
                device_id=self.peer(self.at(sign)),
                device_id_type=MESH,
            )
            copy.start()
            self.live[way, step] = copy

    def finish(self, step):
        for way in (0, 1):
            sign = 1 - 2 * way
            low, high = self.span(way, step)
            self.live[way, step].wait_recv()
            mine = self.region(self.at(sign * (self.half - step)), low, high)
            mine[...] = mine[...] + self.land(way, step - 1, low, high)[...]

    def drain(self):
        for copy in self.live.values():
            copy.wait_send()


def update_kernel(
    n_x, n_z, coords_ref, coords_sm, blocks_ref, b_ref, c_ref, out_ref, gsum_ref,
    cbuf, blocks, table, picked, rows_in, khatri, load, held, dense,
    gpart, gbuf, gfin, land_y, land_x, land_x2, land_y2, part_y, part_x,
    local, ks, kr, ts, tr, fs, fr, zs, zr, cs, cr, gs, gr, hs, hr,
    ys, yr, xs, xr, x2s, x2r, y2s, y2r,
):
    grp, rep = lax.axis_index("grp"), lax.axis_index("rep")
    n_grp = n_x * NC
    my_x, my_c = grp // NC, lax.rem(grp, NC)
    my_z, my_y = rep // NY, lax.rem(rep, NY)
    half_z = n_z // 2
    jblocks = b_ref.shape[0]
    chip_blocks = NC * jblocks

    def z_at(offset):
        return lax.rem(my_z + (offset + 2 * n_z), n_z)

    def z_peer(offset):
        return {"grp": grp, "rep": z_at(offset) * NY + my_y}

    def y_peer(y):
        return {"grp": grp, "rep": my_z * NY + y}

    def x_peer(x):
        return {"grp": x * NC + my_c, "rep": rep}

    def grp_peer(g):
        return {"grp": g, "rep": rep}

    partner = grp_peer(my_x * NC + (1 - my_c))
    own_rows = pl.ds(my_c * jblocks, jblocks)
    fetch_blocks = pltpu.make_async_copy(blocks_ref, blocks, local.at[0])
    fetch_blocks.start()

    @pl.when(my_c == 0)
    def _():
        pltpu.make_async_copy(b_ref, table.at[own_rows], local.at[1]).start()

    @pl.when(my_c != 0)
    def _():
        pltpu.make_async_copy(c_ref, table.at[own_rows], local.at[1]).start()

    barrier = pltpu.get_barrier_semaphore()
    greeted = [grp_peer(lax.rem(grp + k, n_grp)) for k in range(1, n_grp)]
    greeted += [y_peer(lax.rem(my_y + k, NY)) for k in range(1, NY)]
    greeted += [z_peer(k) for k in (1, -1, 2, -2)]
    for who in greeted:
        pl.semaphore_signal(barrier, inc=1, device_id=who, device_id_type=MESH)
    pl.semaphore_wait(barrier, len(greeted))

    sent = []

    def remote(src, dst, send, recv, who):
        copy = pltpu.make_async_remote_copy(
            src_ref=src, dst_ref=dst, send_sem=send, recv_sem=recv,
            device_id=who, device_id_type=MESH,
        )
        copy.start()
        sent.append(copy)
        return copy

    asked = [
        remote(
            coords_ref, cbuf.at[grp], ks.at[k - 1], kr.at[k - 1],
            grp_peer(lax.rem(grp + k, n_grp)),
        )
        for k in range(1, n_grp)
    ]

    def share(ref):
        return pltpu.make_async_remote_copy(
            src_ref=ref, dst_ref=table.at[own_rows], send_sem=ts, recv_sem=tr,
            device_id=partner, device_id_type=MESH,
        )

    @pl.when(my_c == 0)
    def _():
        share(c_ref).start()

    @pl.when(my_c != 0)
    def _():
        share(b_ref).start()

    pltpu.make_async_copy(b_ref, table.at[own_rows], local.at[1]).wait()
    sent.append(share(b_ref))
    share(b_ref).wait_recv()

    def look_up(q):
        return table[lax.rem(q, chip_blocks)]

    answered = []
    for k in range(1, n_grp):
        asked[k - 1].wait_recv()
        asker = lax.rem(grp + (n_grp - k), n_grp)
        for b in range(2):
            picked[k - 1, b] = look_up(cbuf[asker, b, 1 + my_c])
        answered.append(
            remote(
                picked.at[k - 1], rows_in.at[my_x, my_c], fs.at[k - 1], fr.at[k - 1],
                grp_peer(asker),
            )
        )
    for b in range(2):
        rows_in[my_x, my_c, b] = look_up(coords_sm[b, 1 + my_c])

    dims = (((0,), (0,)), ((), ()))
    whole = table[...].reshape(chip_blocks * BS, R)
    gpart[...] = lax.dot_general(whole, whole, dims, preferred_element_type=jnp.float32)
    fetch_blocks.wait()
    for copy in answered:
        copy.wait_recv()

    z_live, c_live = {}, {}

    def carried(distance, way, piece):
        return distance < half_z or piece == way

    def pass_on(distance, way, piece):
        sign = 1 if way == 0 else -1
        hop = min(distance, 2)
        origin = z_at(-sign * (distance - hop))
        src = load.at[piece] if distance <= 2 else held.at[origin, my_c, piece]
        z_live[distance, way, piece] = remote(
            src, held.at[origin, my_c, piece],
            zs.at[way, distance - 1, piece], zr.at[way, distance - 1, piece],
            z_peer(sign * hop),
        )

    def hand_over(offset, piece):
        origin = z_at(offset)
        src = load.at[piece] if offset == 0 else held.at[origin, my_c, piece]
        slot = offset + half_z
        c_live[offset, piece] = remote(
            src, held.at[origin, my_c, piece], cs.at[slot, piece], cr.at[slot, piece], partner
        )

    for piece in range(2):
        left = rows_in[lax.div(coords_sm[piece, 1], chip_blocks), 0, piece].astype(jnp.float32)
        right = rows_in[lax.div(coords_sm[piece, 2], chip_blocks), 1, piece].astype(jnp.float32)
        for j in range(BS):
            khatri[j * BS : (j + 1) * BS, :] = (left[j : j + 1, :] * right).astype(jnp.bfloat16)
        partial = jnp.dot(blocks[piece], khatri[...], preferred_element_type=jnp.float32)
        mark = jnp.full((8, R), coords_sm[piece, 0], jnp.int32).astype(jnp.float32)
        load[piece, 0:BS, :] = partial
        load[piece, BS : BS + 8, :] = mark
        for distance in (2, 1):
            for way in range(2):
                if distance <= half_z and carried(distance, way, piece):
                    pass_on(distance, way, piece)
        hand_over(0, piece)
        held[my_z, my_c, piece, 0:BS, :] = partial
        held[my_z, my_c, piece, BS : BS + 8, :] = mark

    gram_live = [
        remote(
            gpart, gbuf.at[my_x], gs.at[k - 1], gr.at[k - 1], x_peer(lax.rem(my_x + k, n_x))
        )
        for k in range(1, n_x)
    ]
    gbuf[my_x] = gpart[...]

    def absorb(offset, first):
        origin = z_at(offset)
        marks = [held[origin, c, b, BS : BS + 8, :] for c in range(NC) for b in range(2)]
        for part in range(2):
            rows = slice(part * (BS // 2), (part + 1) * (BS // 2))
            parts = [held[origin, c, b, rows, :] for c in range(NC) for b in range(2)]

            def place(slot, carry):
                x, y = slot // NY, lax.rem(slot, NY)
                target = ((x * NC + my_c) * (n_z * NY) + my_z * NY + y).astype(jnp.float32)
                total = None if first else dense[x, y, rows, :]
                for mark, block in zip(marks, parts):
                    hit = jnp.concatenate([mark == target] * (BS // 16), axis=0)
                    term = jnp.where(hit, block, 0.0)
                    total = term if total is None else total + term
                dense[x, y, rows, :] = total
                return carry

            lax.fori_loop(0, n_x * NY, place, 0)

    waiting = [0]
    fresh = True
    for distance in range(1, half_z + 1):
        arrived = []
        for offset in waiting:
            for piece in range(2):
                c_live[offset, piece].wait_recv()
            absorb(offset, fresh)
            fresh = False
        for piece in range(2):
            for way in range(2):
                if not carried(distance, way, piece):
                    continue
                z_live[distance, way, piece].wait_recv()
                onward = distance + 2
                if onward <= half_z and carried(onward, way, piece):
                    pass_on(onward, way, piece)
                offset = -distance if way == 0 or distance == half_z else distance
                hand_over(offset, piece)
                if offset not in arrived:
                    arrived.append(offset)
        waiting = arrived
    for offset in waiting:
        for piece in range(2):
            c_live[offset, piece].wait_recv()
        absorb(offset, fresh)

    def spread(n, me, peer, source, land, send, recv):
        order = sorted(range(1, n), key=lambda k: -min(k, n - k))
        live = []
        for k in order:
            to = lax.rem(me + k, n)
            live.append(remote(source(to), land.at[k - 1], send.at[k - 1], recv.at[k - 1], peer(to)))
        return live

    y_first = spread(
        NY, my_y, y_peer, lambda y: dense.at[:, y, 0:ROWS_Y, :], land_y, ys, yr
    )
    x_first = Ring(
        n_x, my_x, x_peer,
        lambda x, low, high: dense.at[x, :, low:high, :],
        lambda way, step, low, high: land_x.at[way, step, :, low - ROWS_Y : high - ROWS_Y, :],
        xs, xr, (ROWS_Y, BS),
    )
    x_first.start(1)
    for copy in gram_live:
        copy.wait_recv()
    gram = gbuf[0]
    for x in range(1, n_x):
        gram = gram + gbuf[x]
    gsum_ref[my_c] = gram
    gpart_all = gfin.at[0]
    gpart_all[...] = gram
    gram_over = remote(gpart_all, gfin.at[1], hs, hr, partner)
    for step in range(1, x_first.half):
        x_first.finish(step)
        x_first.start(step + 1)
    x_first.finish(x_first.half)
    part_x[...] = dense[my_x, :, ROWS_Y:BS, :]
    y_last = spread(NY, my_y, y_peer, lambda y: part_x.at[y], land_y2, y2s, y2r)
    for copy in y_first:
        copy.wait_recv()
    for x in range(n_x):
        total = dense[x, my_y, 0:ROWS_Y, :]
        for k in range(NY - 1):
            total = total + land_y[k, x]
        part_y[x] = total
    x_last = spread(n_x, my_x, x_peer, lambda x: part_y.at[x], land_x2, x2s, x2r)
    gram_over.wait_recv()
    gsum_ref[1 - my_c] = gfin[1]
    for copy in x_last:
        copy.wait_recv()
    total = part_y[my_x]
    for k in range(n_x - 1):
        total = total + land_x2[k]
    out_ref[0:ROWS_Y, :] = total
    for copy in y_last:
        copy.wait_recv()
    total = part_x[my_y]
    for k in range(NY - 1):
        total = total + land_y2[k]
    out_ref[ROWS_Y:BS, :] = total
    for copy in sent:
        copy.wait_send()
    x_first.drain()


def update(coords, blocks, factor_b, factor_c, n_x, n_z):
    half_z, half_x, n_grp = n_z // 2, n_x // 2, n_x * NC
    vmem = pl.BlockSpec(memory_space=pltpu.VMEM)
    anywhere = pl.BlockSpec(memory_space=pl.ANY)
    dma = pltpu.SemaphoreType.DMA
    rest = BS - ROWS_Y
    f32, bf16 = jnp.float32, jnp.bfloat16
    factor_b, factor_c = factor_b.reshape(-1, BS, R), factor_c.reshape(-1, BS, R)
    jblocks = factor_b.shape[0]
    return pl.pallas_call(
        functools.partial(update_kernel, n_x, n_z),
        out_shape=(
            jax.ShapeDtypeStruct((BS, R), f32),
            jax.ShapeDtypeStruct((2, R, R), f32),
        ),
        in_specs=[vmem, pl.BlockSpec(memory_space=pltpu.SMEM), anywhere, anywhere, anywhere],
        out_specs=(vmem, vmem),
        scratch_shapes=[
            pltpu.SMEM((n_grp,) + coords.shape, jnp.int32),
            pltpu.VMEM(blocks.shape, bf16),
            pltpu.VMEM((NC * jblocks, BS, R), bf16),
            pltpu.VMEM((n_grp - 1, 2, BS, R), bf16),
            pltpu.VMEM((n_x, NC, 2, BS, R), bf16),
            pltpu.VMEM((BS * BS, R), bf16),
            pltpu.VMEM((2, BS + 8, R), f32),
            pltpu.VMEM((n_z, NC, 2, BS + 8, R), f32),
            pltpu.VMEM((n_x, NY, BS, R), f32),
            pltpu.VMEM((R, R), f32),
            pltpu.VMEM((n_x, R, R), f32),
            pltpu.VMEM((2, R, R), f32),
            pltpu.VMEM((NY - 1, n_x, ROWS_Y, R), f32),
            pltpu.VMEM((2, half_x, NY, rest, R), f32),
            pltpu.VMEM((n_x - 1, ROWS_Y, R), f32),
            pltpu.VMEM((NY - 1, rest, R), f32),
            pltpu.VMEM((n_x, ROWS_Y, R), f32),
            pltpu.VMEM((NY, rest, R), f32),
            dma((2,)),
            dma((n_grp - 1,)), dma((n_grp - 1,)),
            dma, dma,
            dma((n_grp - 1,)), dma((n_grp - 1,)),
            dma((2, half_z, 2)), dma((2, half_z, 2)),
            dma((n_z + 1, 2)), dma((n_z + 1, 2)),
            dma((n_x - 1,)), dma((n_x - 1,)),
            dma, dma,
            dma((NY - 1,)), dma((NY - 1,)),
            dma((2, half_x)), dma((2, half_x)),
            dma((n_x - 1,)), dma((n_x - 1,)),
            dma((NY - 1,)), dma((NY - 1,)),
        ],
        compiler_params=pltpu.CompilerParams(collective_id=0, has_side_effects=True),
        name="update",
    )(coords, coords, blocks, factor_b, factor_c)


def sweep_kernel(m_ref, a_ref, g_ref, out_ref):
    gram_b, gram_c = g_ref[0], g_ref[1]
    down = lax.broadcasted_iota(jnp.int32, (R, R), 0)
    across = lax.broadcasted_iota(jnp.int32, (R, R), 1)
    on_diag = down == across

    def diagonals(square):
        kept = jnp.where(on_diag, square, 0.0)
        return jnp.sum(kept, axis=0, keepdims=True), jnp.sum(kept, axis=1, keepdims=True)

    b_row, b_col = diagonals(gram_b)
    c_row, c_col = diagonals(gram_c)
    b_row, b_col = jnp.sqrt(b_row), jnp.sqrt(b_col)
    c_row, c_col = jnp.sqrt(c_row), jnp.sqrt(c_col)
    gram = gram_b / (b_col * b_row) * (gram_c / (c_col * c_row))
    target = m_ref[...] / (b_row * c_row)
    pivot_row, pivot_col = diagonals(gram)
    later = jnp.where(down > across, gram, 0.0)
    known = jnp.dot(
        a_ref[...], later, precision=lax.Precision.HIGHEST, preferred_element_type=jnp.float32
    )
    start = ((target - known) / pivot_row).T
    weight = jnp.where(down > across, gram / pivot_col, 0.0)
    tiles = [start[8 * k : 8 * k + 8, :] for k in range(R // 8)]
    weights = [weight[8 * k : 8 * k + 8, :] for k in range(R // 8)]
    for r in range(R):
        own, sub = r // 8, r % 8
        fixed = jnp.maximum(jnp.broadcast_to(tiles[own][sub : sub + 1, :], (8, BS)), 0.0)
        for k in range(own, R // 8):
            if k == own and sub == 7:
                continue
            scale = jnp.broadcast_to(weights[k][:, r : r + 1], (8, BS))
            tiles[k] = tiles[k] - scale * fixed
    out_ref[...] = jnp.maximum(jnp.concatenate(tiles, axis=0), 0.0).T


def sweep(mttkrp, factor_a, gram):
    vmem = pl.BlockSpec(memory_space=pltpu.VMEM)
    return pl.pallas_call(
        sweep_kernel,
        out_shape=jax.ShapeDtypeStruct((BS, R), jnp.float32),
        in_specs=[vmem] * 3,
        out_specs=vmem,
        name="sweep",
    )(mttkrp, factor_a, gram)


def body(blocks, coords, factor_a, factor_b, factor_c):
    n_x, n_z = lax.axis_size("grp") // NC, lax.axis_size("rep") // NY
    mttkrp, gram = update(coords, blocks, factor_b, factor_c, n_x, n_z)
    return sweep(mttkrp, factor_a, gram)


def solution(mesh):
    placed = (
        P(("grp", "rep"), None, None),
        P(("grp", "rep"), None),
        P(("grp", "rep"), None),
        P("grp", None),
        P("grp", None),
    )
    return jax.shard_map(
        body, mesh=mesh, in_specs=placed, out_specs=P(("grp", "rep"), None), check_vma=False
    )
```

```python
import functools

import jax
import jax.numpy as jnp
from jax import lax
from jax.experimental import pallas as pl
from jax.experimental.pallas import tpu as pltpu
from jax.sharding import PartitionSpec as P

R = 128
BS = 64
NC = 2
NY = 8
ROWS_Z = 32
MESH = pl.DeviceIdType.MESH


class Ring:
    def __init__(self, n, me, peer, region, land, send, recv, rows):
        self.n, self.me, self.peer = n, me, peer
        self.region, self.land = region, land
        self.send, self.recv = send, recv
        self.half = n // 2
        self.rows = rows
        self.live = {}

    def at(self, offset):
        return lax.rem(self.me + (offset + 2 * self.n), self.n)

    def span(self, way, step):
        low, high = self.rows
        middle = low + (high - low) // 16 * 8
        if step == 1:
            return (low, middle) if way == 0 else (middle, high)
        return low, high

    def start(self, step):
        for way in (0, 1):
            sign = 1 - 2 * way
            low, high = self.span(way, step)
            copy = pltpu.make_async_remote_copy(
                src_ref=self.region(self.at(sign * (self.half + 1 - step)), low, high),
                dst_ref=self.land(way, step - 1, low, high),
                send_sem=self.send.at[way, step - 1],
                recv_sem=self.recv.at[way, step - 1],
                device_id=self.peer(self.at(sign)),
                device_id_type=MESH,
            )
            copy.start()
            self.live[way, step] = copy

    def finish(self, step):
        for way in (0, 1):
            sign = 1 - 2 * way
            low, high = self.span(way, step)
            self.live[way, step].wait_recv()
            mine = self.region(self.at(sign * (self.half - step)), low, high)
            mine[...] = mine[...] + self.land(way, step - 1, low, high)[...]

    def drain(self):
        for copy in self.live.values():
            copy.wait_send()


def update_kernel(
    n_x, n_z, coords_ref, coords_sm, blocks_ref, b_ref, c_ref, out_ref, gsum_ref,
    cbuf, blocks, table, picked, rows_in, khatri, load_z, load_y, held_z, held_y, dense_z, dense_y,
    sums_z, sums_y, plan_z, plan_y, sm_z, sm_y,
    gpart, gbuf, gfin, land_xz, land_xy, land_z, land_y,
    local, ks, kr, ts, tr, fs, fr, zs, zr, cs, cr, vs, vr, ds, dr, gs, gr, hs, hr,
    xzs, xzr, xys, xyr, zzs, zzr, yys, yyr,
):
    grp, rep = lax.axis_index("grp"), lax.axis_index("rep")
    n_grp = n_x * NC
    my_x, my_c = grp // NC, lax.rem(grp, NC)
    my_z, my_y = rep // NY, lax.rem(rep, NY)
    jblocks = b_ref.shape[0]
    chip_blocks = NC * jblocks

    def z_peer(z):
        return {"grp": grp, "rep": z * NY + my_y}

    def y_peer(y):
        return {"grp": grp, "rep": my_z * NY + y}

    def x_peer(x):
        return {"grp": x * NC + my_c, "rep": rep}

    def grp_peer(g):
        return {"grp": g, "rep": rep}

    partner = grp_peer(my_x * NC + (1 - my_c))
    own_rows = pl.ds(my_c * jblocks, jblocks)
    fetch_blocks = pltpu.make_async_copy(blocks_ref, blocks, local.at[0])
    fetch_blocks.start()

    @pl.when(my_c == 0)
    def _():
        pltpu.make_async_copy(b_ref, table.at[own_rows], local.at[1]).start()

    @pl.when(my_c != 0)
    def _():
        pltpu.make_async_copy(c_ref, table.at[own_rows], local.at[1]).start()

    barrier = pltpu.get_barrier_semaphore()
    greeted = [grp_peer(lax.rem(grp + k, n_grp)) for k in range(1, n_grp)]
    greeted += [y_peer(lax.rem(my_y + k, NY)) for k in range(1, NY)]
    greeted += [z_peer(lax.rem(my_z + k, n_z)) for k in range(1, n_z)]
    for who in greeted:
        pl.semaphore_signal(barrier, inc=1, device_id=who, device_id_type=MESH)
    for blank in (sums_z, sums_y, plan_z, plan_y):
        blank[...] = jnp.zeros_like(blank)
    pl.semaphore_wait(barrier, len(greeted))

    sent = []

    def remote(src, dst, send, recv, who):
        copy = pltpu.make_async_remote_copy(
            src_ref=src, dst_ref=dst, send_sem=send, recv_sem=recv,
            device_id=who, device_id_type=MESH,
        )
        copy.start()
        sent.append(copy)
        return copy

    asked = [
        remote(
            coords_ref, cbuf.at[grp], ks.at[k - 1], kr.at[k - 1],
            grp_peer(lax.rem(grp + k, n_grp)),
        )
        for k in range(1, n_grp)
    ]

    def share(ref):
        return pltpu.make_async_remote_copy(
            src_ref=ref, dst_ref=table.at[own_rows], send_sem=ts, recv_sem=tr,
            device_id=partner, device_id_type=MESH,
        )

    @pl.when(my_c == 0)
    def _():
        share(c_ref).start()

    @pl.when(my_c != 0)
    def _():
        share(b_ref).start()

    pltpu.make_async_copy(b_ref, table.at[own_rows], local.at[1]).wait()
    sent.append(share(b_ref))
    share(b_ref).wait_recv()

    def look_up(q):
        return table[lax.rem(q, chip_blocks)]

    answered = []
    for k in range(1, n_grp):
        asked[k - 1].wait_recv()
        asker = lax.rem(grp + (n_grp - k), n_grp)
        for b in range(2):
            picked[k - 1, b] = look_up(cbuf[asker, b, 1 + my_c])
        answered.append(
            remote(
                picked.at[k - 1], rows_in.at[my_x, my_c], fs.at[k - 1], fr.at[k - 1],
                grp_peer(asker),
            )
        )
    for b in range(2):
        rows_in[my_x, my_c, b] = look_up(coords_sm[b, 1 + my_c])

    dims = (((0,), (0,)), ((), ()))
    whole = table[...].reshape(chip_blocks * BS, R)
    gpart[...] = lax.dot_general(whole, whole, dims, preferred_element_type=jnp.float32)
    fetch_blocks.wait()
    for copy in answered:
        copy.wait_recv()

    for piece in range(2):
        left = rows_in[lax.div(coords_sm[piece, 1], chip_blocks), 0, piece].astype(jnp.float32)
        right = rows_in[lax.div(coords_sm[piece, 2], chip_blocks), 1, piece].astype(jnp.float32)
        for j in range(BS):
            khatri[j * BS : (j + 1) * BS, :] = (left[j : j + 1, :] * right).astype(jnp.bfloat16)
        partial = jnp.dot(blocks[piece], khatri[...], preferred_element_type=jnp.float32)
        mark = jnp.full((4, R), coords_sm[piece, 0], jnp.int32).astype(jnp.float32)
        for load, low, high in ((load_z, 0, ROWS_Z), (load_y, ROWS_Z, BS)):
            count = high - low
            load[piece * count : (piece + 1) * count, :] = partial[low:high, :]
            load[2 * count + 4 * piece : 2 * count + 4 * piece + 4, :] = mark

    def far_first(n):
        return sorted(range(1, n), key=lambda k: -min(k, n - k))

    def arm(load, held, n, me, peer, send, recv, csend, crecv):
        live, handed = {}, {}

        def give(k):
            live[k] = remote(
                load, held.at[me, my_c], send.at[k - 1], recv.at[k - 1], peer(lax.rem(me + k, n))
            )

        def hand(k):
            origin = lax.rem(me + (n - k), n)
            src = load if k == 0 else held.at[origin, my_c]
            handed[k] = remote(src, held.at[origin, my_c], csend.at[k], crecv.at[k], partner)

        return live, handed, give, hand

    live_z, handed_z, give_z, hand_z = arm(
        load_z, held_z, n_z, my_z, z_peer, zs, zr, cs, cr
    )
    live_y, handed_y, give_y, hand_y = arm(
        load_y, held_y, NY, my_y, y_peer, vs, vr, ds, dr
    )
    order_z, order_y = far_first(n_z), far_first(NY)
    for index in range(max(n_z, NY) - 1):
        if index < n_z - 1:
            give_z(order_z[index])
        if index < NY - 1:
            give_y(order_y[index])
    hand_y(0)
    hand_z(0)
    held_z[my_z, my_c] = load_z[...]
    held_y[my_y, my_c] = load_y[...]

    gram_live = [
        remote(
            gpart, gbuf.at[my_x], gs.at[k - 1], gr.at[k - 1], x_peer(lax.rem(my_x + k, n_x))
        )
        for k in range(1, n_x)
    ]
    gbuf[my_x] = gpart[...]

    def target_z(x, y):
        return (x * NC + my_c) * (n_z * NY) + my_z * NY + y

    def target_y(x, z):
        return (x * NC + my_c) * (n_z * NY) + z * NY + my_y

    def settle(held, sums, dense, plan, plan_sm, sem, n, count, target_of):
        n_slot, n_load = dense.shape[1], n * NC * 2
        lane = lax.broadcasted_iota(jnp.int32, (1, R), 1)
        marks = [
            held[o, c, 2 * count + 4 * b : 2 * count + 4 * b + 1, :]
            for o in range(n) for c in range(NC) for b in range(2)
        ]
        x = sum((lane >= i * n_slot).astype(jnp.int32) for i in range(1, n_x))
        target = target_of(x, lane - x * n_slot).astype(jnp.float32)
        held_by = jnp.zeros((1, R), jnp.float32)
        for k in range(n_load):
            held_by = jnp.where(lane == k, marks[k], held_by)
        first = jnp.full((1, R), n_load, jnp.int32)
        following = jnp.full((1, R), n_load, jnp.int32)
        for k in reversed(range(n_load)):
            first = jnp.where(marks[k] == target, k, first)
            same = jnp.logical_and(marks[k] == held_by, lane < k)
            following = jnp.where(same, k, following)
        plan[0:1, :] = first
        plan[1:2, :] = following
        copy = pltpu.make_async_copy(plan, plan_sm, sem)
        copy.start()
        copy.wait()

        def chain(step, carry):
            o = n - 1 - step
            for c in reversed(range(NC)):
                for b in reversed(range(2)):
                    k = (o * NC + c) * 2 + b
                    block = held[o, c, b * count : (b + 1) * count, :]
                    sums[k] = block + sums[plan_sm[1, k]]
            return carry

        lax.fori_loop(0, n, chain, 0)

        def place(other, carry):
            for x in range(n_x):
                dense[x, other] = sums[plan_sm[0, x * n_slot + other]]
            return carry

        lax.fori_loop(0, n_slot, place, 0)

    def collect(live, handed, hand, order, between):
        for index, k in enumerate(order):
            live[k].wait_recv()
            hand(k)
            if index == len(order) // 2:
                between()
        for copy in handed.values():
            copy.wait_recv()

    def ring(dense, land, send, recv):
        return Ring(
            n_x, my_x, x_peer,
            lambda x, low, high: dense.at[x, :, low:high, :],
            lambda way, step, low, high: land.at[way, step, :, low:high, :],
            send, recv, (0, dense.shape[2]),
        )

    def spread(n, me, peer, source, land, send, recv):
        live = []
        for k in far_first(n):
            to = lax.rem(me + k, n)
            live.append(
                remote(source.at[my_x, to], land.at[k - 1], send.at[k - 1], recv.at[k - 1], peer(to))
            )
        return live

    ring_y = ring(dense_y, land_xy, xys, xyr)
    ring_z = ring(dense_z, land_xz, xzs, xzr)
    collect(live_y, handed_y, hand_y, order_y, lambda: None)
    settle(held_y, sums_y, dense_y, plan_y, sm_y, local.at[2], NY, BS - ROWS_Z, target_y)
    ring_y.start(1)
    for copy in gram_live:
        copy.wait_recv()
    gram = gbuf[0]
    for x in range(1, n_x):
        gram = gram + gbuf[x]
    gsum_ref[my_c] = gram
    gfin[0] = gram
    gram_over = remote(gfin.at[0], gfin.at[1], hs, hr, partner)

    def turn_y():
        for step in range(1, n_x // 2):
            ring_y.finish(step)
            ring_y.start(step + 1)

    collect(live_z, handed_z, hand_z, order_z, turn_y)
    settle(held_z, sums_z, dense_z, plan_z, sm_z, local.at[3], n_z, ROWS_Z, target_z)
    ring_z.start(1)
    for step in range(1, n_x // 2):
        ring_z.finish(step)
        ring_z.start(step + 1)
    ring_y.finish(n_x // 2)
    last_y = spread(n_z, my_z, z_peer, dense_y, land_y, yys, yyr)
    ring_z.finish(n_x // 2)
    last_z = spread(NY, my_y, y_peer, dense_z, land_z, zzs, zzr)
    gram_over.wait_recv()
    gsum_ref[1 - my_c] = gfin[1]
    for live, land, own, low, high in (
        (last_z, land_z, dense_z.at[my_x, my_y], 0, ROWS_Z),
        (last_y, land_y, dense_y.at[my_x, my_z], ROWS_Z, BS),
    ):
        for copy in live:
            copy.wait_recv()
        total = own[...]
        for k in range(len(live)):
            total = total + land[k]
        out_ref[low:high, :] = total
    for copy in sent:
        copy.wait_send()
    ring_y.drain()
    ring_z.drain()


def update(coords, blocks, factor_b, factor_c, n_x, n_z):
    half_x, n_grp = n_x // 2, n_x * NC
    vmem = pl.BlockSpec(memory_space=pltpu.VMEM)
    anywhere = pl.BlockSpec(memory_space=pl.ANY)
    dma = pltpu.SemaphoreType.DMA
    rest = BS - ROWS_Z
    f32, bf16 = jnp.float32, jnp.bfloat16
    factor_b, factor_c = factor_b.reshape(-1, BS, R), factor_c.reshape(-1, BS, R)
    jblocks = factor_b.shape[0]
    return pl.pallas_call(
        functools.partial(update_kernel, n_x, n_z),
        out_shape=(
            jax.ShapeDtypeStruct((BS, R), f32),
            jax.ShapeDtypeStruct((2, R, R), f32),
        ),
        in_specs=[vmem, pl.BlockSpec(memory_space=pltpu.SMEM), anywhere, anywhere, anywhere],
        out_specs=(vmem, vmem),
        scratch_shapes=[
            pltpu.SMEM((n_grp,) + coords.shape, jnp.int32),
            pltpu.VMEM(blocks.shape, bf16),
            pltpu.VMEM((NC * jblocks, BS, R), bf16),
            pltpu.VMEM((n_grp - 1, 2, BS, R), bf16),
            pltpu.VMEM((n_x, NC, 2, BS, R), bf16),
            pltpu.VMEM((BS * BS, R), bf16),
            pltpu.VMEM((2 * ROWS_Z + 8, R), f32),
            pltpu.VMEM((2 * rest + 8, R), f32),
            pltpu.VMEM((n_z, NC, 2 * ROWS_Z + 8, R), f32),
            pltpu.VMEM((NY, NC, 2 * rest + 8, R), f32),
            pltpu.VMEM((n_x, NY, ROWS_Z, R), f32),
            pltpu.VMEM((n_x, n_z, rest, R), f32),
            pltpu.VMEM((n_z * NC * 2 + 1, ROWS_Z, R), f32),
            pltpu.VMEM((NY * NC * 2 + 1, rest, R), f32),
            pltpu.VMEM((8, R), jnp.int32),
            pltpu.VMEM((8, R), jnp.int32),
            pltpu.SMEM((8, R), jnp.int32),
            pltpu.SMEM((8, R), jnp.int32),
            pltpu.VMEM((R, R), f32),
            pltpu.VMEM((n_x, R, R), f32),
            pltpu.VMEM((2, R, R), f32),
            pltpu.VMEM((2, half_x, NY, ROWS_Z, R), f32),
            pltpu.VMEM((2, half_x, n_z, rest, R), f32),
            pltpu.VMEM((NY - 1, ROWS_Z, R), f32),
            pltpu.VMEM((n_z - 1, rest, R), f32),
            dma((4,)),
            dma((n_grp - 1,)), dma((n_grp - 1,)),
            dma, dma,
            dma((n_grp - 1,)), dma((n_grp - 1,)),
            dma((n_z - 1,)), dma((n_z - 1,)),
            dma((n_z,)), dma((n_z,)),
            dma((NY - 1,)), dma((NY - 1,)),
            dma((NY,)), dma((NY,)),
            dma((n_x - 1,)), dma((n_x - 1,)),
            dma, dma,
            dma((2, half_x)), dma((2, half_x)),
            dma((2, half_x)), dma((2, half_x)),
            dma((NY - 1,)), dma((NY - 1,)),
            dma((n_z - 1,)), dma((n_z - 1,)),
        ],
        compiler_params=pltpu.CompilerParams(collective_id=0, has_side_effects=True),
        name="update",
    )(coords, coords, blocks, factor_b, factor_c)


def sweep_kernel(m_ref, a_ref, g_ref, out_ref):
    gram_b, gram_c = g_ref[0], g_ref[1]
    down = lax.broadcasted_iota(jnp.int32, (R, R), 0)
    across = lax.broadcasted_iota(jnp.int32, (R, R), 1)
    on_diag = down == across

    def diagonals(square):
        kept = jnp.where(on_diag, square, 0.0)
        return jnp.sum(kept, axis=0, keepdims=True), jnp.sum(kept, axis=1, keepdims=True)

    b_row, b_col = diagonals(gram_b)
    c_row, c_col = diagonals(gram_c)
    b_row, b_col = jnp.sqrt(b_row), jnp.sqrt(b_col)
    c_row, c_col = jnp.sqrt(c_row), jnp.sqrt(c_col)
    gram = gram_b / (b_col * b_row) * (gram_c / (c_col * c_row))
    target = m_ref[...] / (b_row * c_row)
    pivot_row, pivot_col = diagonals(gram)
    later = jnp.where(down > across, gram, 0.0)
    known = jnp.dot(
        a_ref[...], later, precision=lax.Precision.HIGHEST, preferred_element_type=jnp.float32
    )
    start = ((target - known) / pivot_row).T
    weight = jnp.where(down > across, gram / pivot_col, 0.0)
    tiles = [start[8 * k : 8 * k + 8, :] for k in range(R // 8)]
    weights = [weight[8 * k : 8 * k + 8, :] for k in range(R // 8)]
    for r in range(R):
        own, sub = r // 8, r % 8
        fixed = jnp.maximum(jnp.broadcast_to(tiles[own][sub : sub + 1, :], (8, BS)), 0.0)
        for k in range(own, R // 8):
            if k == own and sub == 7:
                continue
            scale = jnp.broadcast_to(weights[k][:, r : r + 1], (8, BS))
            tiles[k] = tiles[k] - scale * fixed
    out_ref[...] = jnp.maximum(jnp.concatenate(tiles, axis=0), 0.0).T


def sweep(mttkrp, factor_a, gram):
    vmem = pl.BlockSpec(memory_space=pltpu.VMEM)
    return pl.pallas_call(
        sweep_kernel,
        out_shape=jax.ShapeDtypeStruct((BS, R), jnp.float32),
        in_specs=[vmem] * 3,
        out_specs=vmem,
        name="sweep",
    )(mttkrp, factor_a, gram)


def body(blocks, coords, factor_a, factor_b, factor_c):
    n_x, n_z = lax.axis_size("grp") // NC, lax.axis_size("rep") // NY
    mttkrp, gram = update(coords, blocks, factor_b, factor_c, n_x, n_z)
    return sweep(mttkrp, factor_a, gram)


def solution(mesh):
    placed = (
        P(("grp", "rep"), None, None),
        P(("grp", "rep"), None),
        P(("grp", "rep"), None),
        P("grp", None),
        P("grp", None),
    )
    return jax.shard_map(
        body, mesh=mesh, in_specs=placed, out_specs=P(("grp", "rep"), None), check_vma=False
    )
```

```python
import functools

import jax
import jax.numpy as jnp
from jax import lax
from jax.experimental import pallas as pl
from jax.experimental.pallas import tpu as pltpu
from jax.sharding import PartitionSpec as P

R = 128
BS = 64
NC = 2
NY = 8
ROWS_Z = 32
MESH = pl.DeviceIdType.MESH


class Ring:
    def __init__(self, n, me, peer, region, land, send, recv, rows):
        self.n, self.me, self.peer = n, me, peer
        self.region, self.land = region, land
        self.send, self.recv = send, recv
        self.half = n // 2
        self.rows = rows
        self.live = {}

    def at(self, offset):
        return lax.rem(self.me + (offset + 2 * self.n), self.n)

    def span(self, way, step):
        low, high = self.rows
        middle = low + (high - low) // 16 * 8
        if step == 1:
            return (low, middle) if way == 0 else (middle, high)
        return low, high

    def start(self, step):
        for way in (0, 1):
            sign = 1 - 2 * way
            low, high = self.span(way, step)
            copy = pltpu.make_async_remote_copy(
                src_ref=self.region(self.at(sign * (self.half + 1 - step)), low, high),
                dst_ref=self.land(way, step - 1, low, high),
                send_sem=self.send.at[way, step - 1],
                recv_sem=self.recv.at[way, step - 1],
                device_id=self.peer(self.at(sign)),
                device_id_type=MESH,
            )
            copy.start()
            self.live[way, step] = copy

    def finish(self, step):
        for way in (0, 1):
            sign = 1 - 2 * way
            low, high = self.span(way, step)
            self.live[way, step].wait_recv()
            mine = self.region(self.at(sign * (self.half - step)), low, high)
            mine[...] = mine[...] + self.land(way, step - 1, low, high)[...]

    def drain(self):
        for copy in self.live.values():
            copy.wait_send()


def prepare(gram_b, gram_c, a_ref, known, rows, weight_ref):
    down = lax.broadcasted_iota(jnp.int32, (R, R), 0)
    across = lax.broadcasted_iota(jnp.int32, (R, R), 1)

    def diagonals(square):
        kept = jnp.where(down == across, square, 0.0)
        return jnp.sum(kept, axis=0, keepdims=True), jnp.sum(kept, axis=1, keepdims=True)

    b_row, b_col = diagonals(gram_b)
    c_row, c_col = diagonals(gram_c)
    b_row, b_col = jnp.sqrt(b_row), jnp.sqrt(b_col)
    c_row, c_col = jnp.sqrt(c_row), jnp.sqrt(c_col)
    gram = gram_b / (b_col * b_row) * (gram_c / (c_col * c_row))
    pivot_row, pivot_col = diagonals(gram)
    later = jnp.where(down > across, gram, 0.0)
    known[...] = jnp.dot(
        a_ref[...], later, precision=lax.Precision.HIGHEST, preferred_element_type=jnp.float32
    )
    rows[0:1, :] = b_row * c_row
    rows[1:2, :] = pivot_row
    weight_ref[...] = jnp.where(down > across, gram / pivot_col, 0.0)


def update_kernel(
    n_x, n_z, coords_hbm, blocks_ref, b_ref, c_ref, a_hbm, out_ref, weight_ref,
    coords_ref, coords_sm, a_ref, cbuf, blocks, table, picked, rows_in, khatri, load_z, load_y, held_z, held_y, dense_z, dense_y,
    sums_z, sums_y, plan_z, plan_y, sm_z, sm_y,
    gpart, gbuf, gfin, gsum, known, rows, land_xz, land_xy, land_z, land_y,
    local, ks, kr, ts, tr, fs, fr, zs, zr, cs, cr, vs, vr, ds, dr, gs, gr, hs, hr,
    xzs, xzr, xys, xyr, zzs, zzr, yys, yyr,
):
    grp, rep = lax.axis_index("grp"), lax.axis_index("rep")
    n_grp = n_x * NC
    my_x, my_c = grp // NC, lax.rem(grp, NC)
    my_z, my_y = rep // NY, lax.rem(rep, NY)
    jblocks = b_ref.shape[0]
    chip_blocks = NC * jblocks

    def z_peer(z):
        return {"grp": grp, "rep": z * NY + my_y}

    def y_peer(y):
        return {"grp": grp, "rep": my_z * NY + y}

    def x_peer(x):
        return {"grp": x * NC + my_c, "rep": rep}

    def grp_peer(g):
        return {"grp": g, "rep": rep}

    partner = grp_peer(my_x * NC + (1 - my_c))
    own_rows = pl.ds(my_c * jblocks, jblocks)
    fetch_blocks = pltpu.make_async_copy(blocks_ref, blocks, local.at[0])
    fetch_coords = pltpu.make_async_copy(coords_hbm, coords_ref, local.at[4])
    fetch_own = pltpu.make_async_copy(coords_hbm, coords_sm, local.at[5])
    fetch_a = pltpu.make_async_copy(a_hbm, a_ref, local.at[6])

    def own_part():
        @pl.when(my_c == 0)
        def _():
            pltpu.make_async_copy(b_ref, table.at[own_rows], local.at[1]).start()

        @pl.when(my_c != 0)
        def _():
            pltpu.make_async_copy(c_ref, table.at[own_rows], local.at[1]).start()

    barrier = pltpu.get_barrier_semaphore()
    greeted = [grp_peer(lax.rem(grp + k, n_grp)) for k in range(1, n_grp)]
    greeted += [y_peer(lax.rem(my_y + k, NY)) for k in range(1, NY)]
    greeted += [z_peer(lax.rem(my_z + k, n_z)) for k in range(1, n_z)]
    for who in greeted:
        pl.semaphore_signal(barrier, inc=1, device_id=who, device_id_type=MESH)
    for copy in (fetch_coords, fetch_own, fetch_blocks, fetch_a):
        copy.start()
    own_part()
    for blank in (sums_z, sums_y, plan_z, plan_y):
        blank[...] = jnp.zeros_like(blank)
    fetch_coords.wait()
    fetch_own.wait()
    pl.semaphore_wait(barrier, len(greeted))

    sent = []

    def remote(src, dst, send, recv, who):
        copy = pltpu.make_async_remote_copy(
            src_ref=src, dst_ref=dst, send_sem=send, recv_sem=recv,
            device_id=who, device_id_type=MESH,
        )
        copy.start()
        sent.append(copy)
        return copy

    def far_first(n):
        return sorted(range(1, n), key=lambda k: -min(k, n - k))

    order_g = far_first(n_grp)
    asked = {
        k: remote(
            coords_ref, cbuf.at[grp], ks.at[k - 1], kr.at[k - 1],
            grp_peer(lax.rem(grp + k, n_grp)),
        )
        for k in order_g
    }

    def share(ref):
        return pltpu.make_async_remote_copy(
            src_ref=ref, dst_ref=table.at[own_rows], send_sem=ts, recv_sem=tr,
            device_id=partner, device_id_type=MESH,
        )

    @pl.when(my_c == 0)
    def _():
        share(c_ref).start()

    @pl.when(my_c != 0)
    def _():
        share(b_ref).start()

    pltpu.make_async_copy(b_ref, table.at[own_rows], local.at[1]).wait()
    sent.append(share(b_ref))
    share(b_ref).wait_recv()

    def look_up(q):
        return table[lax.rem(q, chip_blocks)]

    answered = []
    for k in order_g:
        asked[k].wait_recv()
        asker = lax.rem(grp + (n_grp - k), n_grp)
        for b in range(2):
            picked[k - 1, b] = look_up(cbuf[asker, b, 1 + my_c])
        answered.append(
            remote(
                picked.at[k - 1], rows_in.at[my_x, my_c], fs.at[k - 1], fr.at[k - 1],
                grp_peer(asker),
            )
        )
    for b in range(2):
        rows_in[my_x, my_c, b] = look_up(coords_sm[b, 1 + my_c])

    fetch_blocks.wait()
    for copy in answered:
        copy.wait_recv()

    for piece in range(2):
        left = rows_in[lax.div(coords_sm[piece, 1], chip_blocks), 0, piece].astype(jnp.float32)
        right = rows_in[lax.div(coords_sm[piece, 2], chip_blocks), 1, piece].astype(jnp.float32)
        for j in range(BS):
            khatri[j * BS : (j + 1) * BS, :] = (left[j : j + 1, :] * right).astype(jnp.bfloat16)
        partial = jnp.dot(blocks[piece], khatri[...], preferred_element_type=jnp.float32)
        mark = jnp.full((4, R), coords_sm[piece, 0], jnp.int32).astype(jnp.float32)
        for load, low, high in ((load_z, 0, ROWS_Z), (load_y, ROWS_Z, BS)):
            count = high - low
            load[piece * count : (piece + 1) * count, :] = partial[low:high, :]
            load[2 * count + 4 * piece : 2 * count + 4 * piece + 4, :] = mark

    def arm(load, held, n, me, peer, send, recv, csend, crecv):
        live, handed = {}, {}

        def give(k):
            live[k] = remote(
                load, held.at[me, my_c], send.at[k - 1], recv.at[k - 1], peer(lax.rem(me + k, n))
            )

        def hand(k):
            origin = lax.rem(me + (n - k), n)
            src = load if k == 0 else held.at[origin, my_c]
            handed[k] = remote(src, held.at[origin, my_c], csend.at[k], crecv.at[k], partner)

        return live, handed, give, hand

    live_z, handed_z, give_z, hand_z = arm(
        load_z, held_z, n_z, my_z, z_peer, zs, zr, cs, cr
    )
    live_y, handed_y, give_y, hand_y = arm(
        load_y, held_y, NY, my_y, y_peer, vs, vr, ds, dr
    )
    order_z, order_y = far_first(n_z), far_first(NY)
    for index in range(max(n_z, NY) - 1):
        if index < n_z - 1:
            give_z(order_z[index])
        if index < NY - 1:
            give_y(order_y[index])
    hand_y(0)
    hand_z(0)
    held_z[my_z, my_c] = load_z[...]
    held_y[my_y, my_c] = load_y[...]

    dims = (((0,), (0,)), ((), ()))
    whole = table[...].reshape(chip_blocks * BS, R)
    gpart[...] = lax.dot_general(whole, whole, dims, preferred_element_type=jnp.float32)
    gram_live = [
        remote(
            gpart, gbuf.at[my_x], gs.at[k - 1], gr.at[k - 1], x_peer(lax.rem(my_x + k, n_x))
        )
        for k in range(1, n_x)
    ]
    gbuf[my_x] = gpart[...]

    def target_z(x, y):
        return (x * NC + my_c) * (n_z * NY) + my_z * NY + y

    def target_y(x, z):
        return (x * NC + my_c) * (n_z * NY) + z * NY + my_y

    def settle(held, sums, dense, plan, plan_sm, sem, n, count, target_of):
        n_slot, n_load = dense.shape[1], n * NC * 2
        lane = lax.broadcasted_iota(jnp.int32, (1, R), 1)
        marks = [
            held[o, c, 2 * count + 4 * b : 2 * count + 4 * b + 1, :]
            for o in range(n) for c in range(NC) for b in range(2)
        ]
        x = sum((lane >= i * n_slot).astype(jnp.int32) for i in range(1, n_x))
        target = target_of(x, lane - x * n_slot).astype(jnp.float32)
        held_by = jnp.zeros((1, R), jnp.float32)
        for k in range(n_load):
            held_by = jnp.where(lane == k, marks[k], held_by)
        first = jnp.full((1, R), n_load, jnp.int32)
        following = jnp.full((1, R), n_load, jnp.int32)
        for k in reversed(range(n_load)):
            first = jnp.where(marks[k] == target, k, first)
            same = jnp.logical_and(marks[k] == held_by, lane < k)
            following = jnp.where(same, k, following)
        plan[0:1, :] = first
        plan[1:2, :] = following
        copy = pltpu.make_async_copy(plan, plan_sm, sem)
        copy.start()
        copy.wait()

        def chain(step, carry):
            o = n - 1 - step
            for c in reversed(range(NC)):
                for b in reversed(range(2)):
                    k = (o * NC + c) * 2 + b
                    block = held[o, c, b * count : (b + 1) * count, :]
                    sums[k] = block + sums[plan_sm[1, k]]
            return carry

        lax.fori_loop(0, n, chain, 0)

        def place(other, carry):
            for x in range(n_x):
                dense[x, other] = sums[plan_sm[0, x * n_slot + other]]
            return carry

        lax.fori_loop(0, n_slot, place, 0)

    def collect(live, handed, hand, order, between):
        for index, k in enumerate(order):
            live[k].wait_recv()
            hand(k)
            if index == len(order) // 2:
                between()
        for copy in handed.values():
            copy.wait_recv()

    def ring(dense, land, send, recv):
        return Ring(
            n_x, my_x, x_peer,
            lambda x, low, high: dense.at[x, :, low:high, :],
            lambda way, step, low, high: land.at[way, step, :, low:high, :],
            send, recv, (0, dense.shape[2]),
        )

    def spread(n, me, peer, source, land, send, recv):
        live = []
        for k in far_first(n):
            to = lax.rem(me + k, n)
            live.append(
                remote(source.at[my_x, to], land.at[k - 1], send.at[k - 1], recv.at[k - 1], peer(to))
            )
        return live

    ring_y = ring(dense_y, land_xy, xys, xyr)
    ring_z = ring(dense_z, land_xz, xzs, xzr)
    collect(live_y, handed_y, hand_y, order_y, lambda: None)
    settle(held_y, sums_y, dense_y, plan_y, sm_y, local.at[2], NY, BS - ROWS_Z, target_y)
    ring_y.start(1)
    for copy in gram_live:
        copy.wait_recv()
    gram = gbuf[0]
    for x in range(1, n_x):
        gram = gram + gbuf[x]
    gsum[my_c] = gram
    gfin[0] = gram
    gram_over = remote(gfin.at[0], gfin.at[1], hs, hr, partner)

    def turn_y():
        for step in range(1, n_x // 2):
            ring_y.finish(step)
            ring_y.start(step + 1)
        gram_over.wait_recv()
        gsum[1 - my_c] = gfin[1]
        fetch_a.wait()
        prepare(gsum[0], gsum[1], a_ref, known, rows, weight_ref)

    collect(live_z, handed_z, hand_z, order_z, turn_y)
    settle(held_z, sums_z, dense_z, plan_z, sm_z, local.at[3], n_z, ROWS_Z, target_z)
    ring_z.start(1)
    ring_y.finish(n_x // 2)
    last_y = spread(n_z, my_z, z_peer, dense_y, land_y, yys, yyr)
    for step in range(1, n_x // 2):
        ring_z.finish(step)
        ring_z.start(step + 1)
    ring_z.finish(n_x // 2)
    last_z = spread(NY, my_y, y_peer, dense_z, land_z, zzs, zzr)
    for live, land, own, low, high in (
        (last_y, land_y, dense_y.at[my_x, my_z], ROWS_Z, BS),
        (last_z, land_z, dense_z.at[my_x, my_y], 0, ROWS_Z),
    ):
        for copy in live:
            copy.wait_recv()
        total = own[...]
        for k in range(len(live)):
            total = total + land[k]
        out_ref[low:high, :] = (total / rows[0:1, :] - known[low:high, :]) / rows[1:2, :]
    for copy in sent:
        copy.wait_send()
    ring_y.drain()
    ring_z.drain()


def update(coords, blocks, factor_b, factor_c, factor_a, n_x, n_z):
    half_x, n_grp = n_x // 2, n_x * NC
    vmem = pl.BlockSpec(memory_space=pltpu.VMEM)
    anywhere = pl.BlockSpec(memory_space=pl.ANY)
    dma = pltpu.SemaphoreType.DMA
    rest = BS - ROWS_Z
    f32, bf16 = jnp.float32, jnp.bfloat16
    factor_b, factor_c = factor_b.reshape(-1, BS, R), factor_c.reshape(-1, BS, R)
    jblocks = factor_b.shape[0]
    return pl.pallas_call(
        functools.partial(update_kernel, n_x, n_z),
        out_shape=(
            jax.ShapeDtypeStruct((BS, R), f32),
            jax.ShapeDtypeStruct((R, R), f32),
        ),
        in_specs=[anywhere] * 5,
        out_specs=(vmem, vmem),
        scratch_shapes=[
            pltpu.VMEM(coords.shape, jnp.int32),
            pltpu.SMEM(coords.shape, jnp.int32),
            pltpu.VMEM((BS, R), f32),
            pltpu.SMEM((n_grp,) + coords.shape, jnp.int32),
            pltpu.VMEM(blocks.shape, bf16),
            pltpu.VMEM((NC * jblocks, BS, R), bf16),
            pltpu.VMEM((n_grp - 1, 2, BS, R), bf16),
            pltpu.VMEM((n_x, NC, 2, BS, R), bf16),
            pltpu.VMEM((BS * BS, R), bf16),
            pltpu.VMEM((2 * ROWS_Z + 8, R), f32),
            pltpu.VMEM((2 * rest + 8, R), f32),
            pltpu.VMEM((n_z, NC, 2 * ROWS_Z + 8, R), f32),
            pltpu.VMEM((NY, NC, 2 * rest + 8, R), f32),
            pltpu.VMEM((n_x, NY, ROWS_Z, R), f32),
            pltpu.VMEM((n_x, n_z, rest, R), f32),
            pltpu.VMEM((n_z * NC * 2 + 1, ROWS_Z, R), f32),
            pltpu.VMEM((NY * NC * 2 + 1, rest, R), f32),
            pltpu.VMEM((8, R), jnp.int32),
            pltpu.VMEM((8, R), jnp.int32),
            pltpu.SMEM((8, R), jnp.int32),
            pltpu.SMEM((8, R), jnp.int32),
            pltpu.VMEM((R, R), f32),
            pltpu.VMEM((n_x, R, R), f32),
            pltpu.VMEM((2, R, R), f32),
            pltpu.VMEM((2, R, R), f32),
            pltpu.VMEM((BS, R), f32),
            pltpu.VMEM((8, R), f32),
            pltpu.VMEM((2, half_x, NY, ROWS_Z, R), f32),
            pltpu.VMEM((2, half_x, n_z, rest, R), f32),
            pltpu.VMEM((NY - 1, ROWS_Z, R), f32),
            pltpu.VMEM((n_z - 1, rest, R), f32),
            dma((7,)),
            dma((n_grp - 1,)), dma((n_grp - 1,)),
            dma, dma,
            dma((n_grp - 1,)), dma((n_grp - 1,)),
            dma((n_z - 1,)), dma((n_z - 1,)),
            dma((n_z,)), dma((n_z,)),
            dma((NY - 1,)), dma((NY - 1,)),
            dma((NY,)), dma((NY,)),
            dma((n_x - 1,)), dma((n_x - 1,)),
            dma, dma,
            dma((2, half_x)), dma((2, half_x)),
            dma((2, half_x)), dma((2, half_x)),
            dma((NY - 1,)), dma((NY - 1,)),
            dma((n_z - 1,)), dma((n_z - 1,)),
        ],
        compiler_params=pltpu.CompilerParams(collective_id=0, has_side_effects=True),
        name="update",
    )(coords, blocks, factor_b, factor_c, factor_a)


def sweep_kernel(start_ref, weight_ref, out_ref):
    start, weight = start_ref[...].T, weight_ref[...]
    tiles = [start[8 * k : 8 * k + 8, :] for k in range(R // 8)]
    weights = [weight[8 * k : 8 * k + 8, :] for k in range(R // 8)]
    for r in range(R):
        own, sub = r // 8, r % 8
        fixed = jnp.maximum(jnp.broadcast_to(tiles[own][sub : sub + 1, :], (8, BS)), 0.0)
        for k in range(own, R // 8):
            if k == own and sub == 7:
                continue
            scale = jnp.broadcast_to(weights[k][:, r : r + 1], (8, BS))
            tiles[k] = tiles[k] - scale * fixed
    out_ref[...] = jnp.maximum(jnp.concatenate(tiles, axis=0), 0.0).T


def sweep(start, weight):
    vmem = pl.BlockSpec(memory_space=pltpu.VMEM)
    return pl.pallas_call(
        sweep_kernel,
        out_shape=jax.ShapeDtypeStruct((BS, R), jnp.float32),
        in_specs=[vmem] * 2,
        out_specs=vmem,
        name="sweep",
    )(start, weight)


def body(blocks, coords, factor_a, factor_b, factor_c):
    n_x, n_z = lax.axis_size("grp") // NC, lax.axis_size("rep") // NY
    start, weight = update(coords, blocks, factor_b, factor_c, factor_a, n_x, n_z)
    return sweep(start, weight)


def solution(mesh):
    placed = (
        P(("grp", "rep"), None, None),
        P(("grp", "rep"), None),
        P(("grp", "rep"), None),
        P("grp", None),
        P("grp", None),
    )
    return jax.shard_map(
        body, mesh=mesh, in_specs=placed, out_specs=P(("grp", "rep"), None), check_vma=False
    )
```

```python
import functools

import jax
import jax.numpy as jnp
from jax import lax
from jax.experimental import pallas as pl
from jax.experimental.pallas import tpu as pltpu
from jax.sharding import PartitionSpec as P

R = 128
BS = 64
NC = 2
NY = 8
ROWS_Z = 32
MESH = pl.DeviceIdType.MESH


class Ring:
    def __init__(self, n, me, peer, region, land, send, recv, rows):
        self.n, self.me, self.peer = n, me, peer
        self.region, self.land = region, land
        self.send, self.recv = send, recv
        self.half = n // 2
        self.rows = rows
        self.live = {}

    def at(self, offset):
        return lax.rem(self.me + (offset + 2 * self.n), self.n)

    def span(self, way, step):
        low, high = self.rows
        middle = low + (high - low) // 16 * 8
        if step == 1:
            return (low, middle) if way == 0 else (middle, high)
        return low, high

    def start(self, step):
        for way in (0, 1):
            sign = 1 - 2 * way
            low, high = self.span(way, step)
            copy = pltpu.make_async_remote_copy(
                src_ref=self.region(self.at(sign * (self.half + 1 - step)), low, high),
                dst_ref=self.land(way, step - 1, low, high),
                send_sem=self.send.at[way, step - 1],
                recv_sem=self.recv.at[way, step - 1],
                device_id=self.peer(self.at(sign)),
                device_id_type=MESH,
            )
            copy.start()
            self.live[way, step] = copy

    def finish(self, step):
        for way in (0, 1):
            sign = 1 - 2 * way
            low, high = self.span(way, step)
            self.live[way, step].wait_recv()
            mine = self.region(self.at(sign * (self.half - step)), low, high)
            mine[...] = mine[...] + self.land(way, step - 1, low, high)[...]

    def drain(self):
        for copy in self.live.values():
            copy.wait_send()


def prepare(gram_b, gram_c, a_ref, known, rows, weight_ref):
    down = lax.broadcasted_iota(jnp.int32, (R, R), 0)
    across = lax.broadcasted_iota(jnp.int32, (R, R), 1)

    def diagonals(square):
        kept = jnp.where(down == across, square, 0.0)
        return jnp.sum(kept, axis=0, keepdims=True), jnp.sum(kept, axis=1, keepdims=True)

    b_row, b_col = diagonals(gram_b)
    c_row, c_col = diagonals(gram_c)
    b_row, b_col = jnp.sqrt(b_row), jnp.sqrt(b_col)
    c_row, c_col = jnp.sqrt(c_row), jnp.sqrt(c_col)
    gram = gram_b / (b_col * b_row) * (gram_c / (c_col * c_row))
    pivot_row, pivot_col = diagonals(gram)
    later = jnp.where(down > across, gram, 0.0)
    known[...] = jnp.dot(
        a_ref[...], later, precision=lax.Precision.HIGHEST, preferred_element_type=jnp.float32
    )
    rows[0:1, :] = b_row * c_row
    rows[1:2, :] = pivot_row
    weight_ref[...] = jnp.where(down > across, gram / pivot_col, 0.0)


def update_kernel(
    n_x, n_z, coords_hbm, blocks_ref, b_ref, c_ref, a_hbm, out_ref, weight_ref,
    coords_ref, coords_sm, a_ref, cbuf, blocks, table, picked, rows_in, khatri, load_z, load_y, held_z, held_y, dense_z, dense_y,
    sums_z, sums_y, plan_z, plan_y, sm_z, sm_y,
    gpart, gbuf, gfin, gsum, known, rows, land_xz, land_xy, land_z, land_y,
    local, ks, kr, ts, tr, fs, fr, zs, zr, cs, cr, vs, vr, ds, dr, gs, gr, hs, hr,
    xzs, xzr, xys, xyr, zzs, zzr, yys, yyr,
):
    grp, rep = lax.axis_index("grp"), lax.axis_index("rep")
    n_grp = n_x * NC
    my_x, my_c = grp // NC, lax.rem(grp, NC)
    my_z, my_y = rep // NY, lax.rem(rep, NY)
    jblocks = b_ref.shape[0]
    chip_blocks = NC * jblocks

    def z_peer(z):
        return {"grp": grp, "rep": z * NY + my_y}

    def y_peer(y):
        return {"grp": grp, "rep": my_z * NY + y}

    def x_peer(x):
        return {"grp": x * NC + my_c, "rep": rep}

    def grp_peer(g):
        return {"grp": g, "rep": rep}

    partner = grp_peer(my_x * NC + (1 - my_c))
    own_rows = pl.ds(my_c * jblocks, jblocks)
    fetch_blocks = pltpu.make_async_copy(blocks_ref, blocks, local.at[0])
    fetch_coords = pltpu.make_async_copy(coords_hbm, coords_ref, local.at[4])
    fetch_own = pltpu.make_async_copy(coords_hbm, coords_sm, local.at[5])
    fetch_a = pltpu.make_async_copy(a_hbm, a_ref, local.at[6])

    def own_part():
        @pl.when(my_c == 0)
        def _():
            pltpu.make_async_copy(b_ref, table.at[own_rows], local.at[1]).start()

        @pl.when(my_c != 0)
        def _():
            pltpu.make_async_copy(c_ref, table.at[own_rows], local.at[1]).start()

    barrier = pltpu.get_barrier_semaphore()
    greeted = [grp_peer(lax.rem(grp + k, n_grp)) for k in range(1, n_grp)]
    greeted += [y_peer(lax.rem(my_y + k, NY)) for k in range(1, NY)]
    greeted += [z_peer(lax.rem(my_z + k, n_z)) for k in range(1, n_z)]
    for who in greeted:
        pl.semaphore_signal(barrier, inc=1, device_id=who, device_id_type=MESH)
    for copy in (fetch_coords, fetch_own, fetch_blocks, fetch_a):
        copy.start()
    own_part()
    for blank in (sums_z, sums_y, plan_z, plan_y):
        blank[...] = jnp.zeros_like(blank)
    fetch_coords.wait()
    fetch_own.wait()
    pl.semaphore_wait(barrier, len(greeted))

    sent = []

    def remote(src, dst, send, recv, who):
        copy = pltpu.make_async_remote_copy(
            src_ref=src, dst_ref=dst, send_sem=send, recv_sem=recv,
            device_id=who, device_id_type=MESH,
        )
        copy.start()
        sent.append(copy)
        return copy

    def far_first(n):
        return sorted(range(1, n), key=lambda k: -min(k, n - k))

    order_g = far_first(n_grp)
    asked = {
        k: remote(
            coords_ref, cbuf.at[grp], ks.at[k - 1], kr.at[k - 1],
            grp_peer(lax.rem(grp + k, n_grp)),
        )
        for k in order_g
    }

    def share(ref):
        return pltpu.make_async_remote_copy(
            src_ref=ref, dst_ref=table.at[own_rows], send_sem=ts, recv_sem=tr,
            device_id=partner, device_id_type=MESH,
        )

    @pl.when(my_c == 0)
    def _():
        share(c_ref).start()

    @pl.when(my_c != 0)
    def _():
        share(b_ref).start()

    pltpu.make_async_copy(b_ref, table.at[own_rows], local.at[1]).wait()
    sent.append(share(b_ref))
    share(b_ref).wait_recv()

    def look_up(q):
        return table[lax.rem(q, chip_blocks)]

    answered = []
    for k in order_g:
        asked[k].wait_recv()
        asker = lax.rem(grp + (n_grp - k), n_grp)
        for b in range(2):
            picked[k - 1, b] = look_up(cbuf[asker, b, 1 + my_c])
        answered.append(
            remote(
                picked.at[k - 1], rows_in.at[my_x, my_c], fs.at[k - 1], fr.at[k - 1],
                grp_peer(asker),
            )
        )
    for b in range(2):
        rows_in[my_x, my_c, b] = look_up(coords_sm[b, 1 + my_c])

    fetch_blocks.wait()
    for copy in answered:
        copy.wait_recv()

    for piece in range(2):
        left = rows_in[lax.div(coords_sm[piece, 1], chip_blocks), 0, piece].astype(jnp.float32)
        right = rows_in[lax.div(coords_sm[piece, 2], chip_blocks), 1, piece].astype(jnp.float32)
        for j in range(BS):
            khatri[j * BS : (j + 1) * BS, :] = (left[j : j + 1, :] * right).astype(jnp.bfloat16)
        partial = jnp.dot(blocks[piece], khatri[...], preferred_element_type=jnp.float32)
        mark = jnp.full((4, R), coords_sm[piece, 0], jnp.int32).astype(jnp.float32)
        for load, low, high in ((load_z, 0, ROWS_Z), (load_y, ROWS_Z, BS)):
            count = high - low
            load[piece * count : (piece + 1) * count, :] = partial[low:high, :]
            load[2 * count + 4 * piece : 2 * count + 4 * piece + 4, :] = mark

    def arm(load, held, n, me, peer, send, recv, csend, crecv):
        live, handed = {}, {}

        def give(k):
            live[k] = remote(
                load, held.at[me, my_c], send.at[k - 1], recv.at[k - 1], peer(lax.rem(me + k, n))
            )

        def hand(k):
            origin = lax.rem(me + (n - k), n)
            src = load if k == 0 else held.at[origin, my_c]
            handed[k] = remote(src, held.at[origin, my_c], csend.at[k], crecv.at[k], partner)

        return live, handed, give, hand

    live_z, handed_z, give_z, hand_z = arm(
        load_z, held_z, n_z, my_z, z_peer, zs, zr, cs, cr
    )
    live_y, handed_y, give_y, hand_y = arm(
        load_y, held_y, NY, my_y, y_peer, vs, vr, ds, dr
    )
    order_z, order_y = far_first(n_z), far_first(NY)
    for index in range(max(n_z, NY) - 1):
        if index < n_z - 1:
            give_z(order_z[index])
        if index < NY - 1:
            give_y(order_y[index])
    hand_y(0)
    hand_z(0)
    held_z[my_z, my_c] = load_z[...]
    held_y[my_y, my_c] = load_y[...]

    dims = (((0,), (0,)), ((), ()))
    whole = table[...].reshape(chip_blocks * BS, R)
    gpart[...] = lax.dot_general(whole, whole, dims, preferred_element_type=jnp.float32)
    gram_live = [
        remote(
            gpart, gbuf.at[my_x], gs.at[k - 1], gr.at[k - 1], x_peer(lax.rem(my_x + k, n_x))
        )
        for k in range(1, n_x)
    ]
    gbuf[my_x] = gpart[...]

    def target_z(x, y):
        return (x * NC + my_c) * (n_z * NY) + my_z * NY + y

    def target_y(x, z):
        return (x * NC + my_c) * (n_z * NY) + z * NY + my_y

    def settle(held, sums, dense, plan, plan_sm, sem, n, count, target_of):
        n_slot, n_load = dense.shape[1], n * NC * 2
        lane = lax.broadcasted_iota(jnp.int32, (1, R), 1)
        marks = [
            held[o, c, 2 * count + 4 * b : 2 * count + 4 * b + 1, :]
            for o in range(n) for c in range(NC) for b in range(2)
        ]
        x = sum((lane >= i * n_slot).astype(jnp.int32) for i in range(1, n_x))
        target = target_of(x, lane - x * n_slot).astype(jnp.float32)
        held_by = jnp.zeros((1, R), jnp.float32)
        for k in range(n_load):
            held_by = jnp.where(lane == k, marks[k], held_by)
        first = jnp.full((1, R), n_load, jnp.int32)
        following = jnp.full((1, R), n_load, jnp.int32)
        for k in reversed(range(n_load)):
            first = jnp.where(marks[k] == target, k, first)
            same = jnp.logical_and(marks[k] == held_by, lane < k)
            following = jnp.where(same, k, following)
        plan[0:1, :] = first
        plan[1:2, :] = following
        copy = pltpu.make_async_copy(plan, plan_sm, sem)
        copy.start()
        copy.wait()

        def chain(step, carry):
            o = n - 1 - step
            for c in reversed(range(NC)):
                for b in reversed(range(2)):
                    k = (o * NC + c) * 2 + b
                    block = held[o, c, b * count : (b + 1) * count, :]
                    sums[k] = block + sums[plan_sm[1, k]]
            return carry

        lax.fori_loop(0, n, chain, 0)

        def place(steps):
            def slot(other, carry):
                for step in steps:
                    x = lax.rem(my_x + step, n_x)
                    dense[x, other] = sums[plan_sm[0, x * n_slot + other]]
                return carry

            lax.fori_loop(0, n_slot, slot, 0)

        place([n_x // 2])
        return lambda: place([step for step in range(n_x) if step != n_x // 2])

    def collect(live, handed, hand, order, between):
        for index, k in enumerate(order):
            live[k].wait_recv()
            hand(k)
            if index == len(order) // 2:
                between()
        for copy in handed.values():
            copy.wait_recv()

    def ring(dense, land, send, recv):
        return Ring(
            n_x, my_x, x_peer,
            lambda x, low, high: dense.at[x, :, low:high, :],
            lambda way, step, low, high: land.at[way, step, :, low:high, :],
            send, recv, (0, dense.shape[2]),
        )

    def spread(n, me, peer, source, land, send, recv):
        live = []
        for k in far_first(n):
            to = lax.rem(me + k, n)
            live.append(
                remote(source.at[my_x, to], land.at[k - 1], send.at[k - 1], recv.at[k - 1], peer(to))
            )
        return live

    ring_y = ring(dense_y, land_xy, xys, xyr)
    ring_z = ring(dense_z, land_xz, xzs, xzr)
    collect(live_y, handed_y, hand_y, order_y, lambda: None)
    rest_y = settle(held_y, sums_y, dense_y, plan_y, sm_y, local.at[2], NY, BS - ROWS_Z, target_y)
    ring_y.start(1)
    rest_y()
    for copy in gram_live:
        copy.wait_recv()
    gram = gbuf[0]
    for x in range(1, n_x):
        gram = gram + gbuf[x]
    gsum[my_c] = gram
    gfin[0] = gram
    gram_over = remote(gfin.at[0], gfin.at[1], hs, hr, partner)

    def turn_y():
        for step in range(1, n_x // 2):
            ring_y.finish(step)
            ring_y.start(step + 1)

    collect(live_z, handed_z, hand_z, order_z, turn_y)
    rest_z = settle(held_z, sums_z, dense_z, plan_z, sm_z, local.at[3], n_z, ROWS_Z, target_z)
    ring_z.start(1)
    rest_z()
    ring_y.finish(n_x // 2)
    last_y = spread(n_z, my_z, z_peer, dense_y, land_y, yys, yyr)
    gram_over.wait_recv()
    gsum[1 - my_c] = gfin[1]
    fetch_a.wait()
    prepare(gsum[0], gsum[1], a_ref, known, rows, weight_ref)
    for step in range(1, n_x // 2):
        ring_z.finish(step)
        ring_z.start(step + 1)
    ring_z.finish(n_x // 2)
    last_z = spread(NY, my_y, y_peer, dense_z, land_z, zzs, zzr)
    for live, land, own, low, high in (
        (last_y, land_y, dense_y.at[my_x, my_z], ROWS_Z, BS),
        (last_z, land_z, dense_z.at[my_x, my_y], 0, ROWS_Z),
    ):
        for copy in live:
            copy.wait_recv()
        total = own[...]
        for k in range(len(live)):
            total = total + land[k]
        out_ref[low:high, :] = (total / rows[0:1, :] - known[low:high, :]) / rows[1:2, :]
    for copy in sent:
        copy.wait_send()
    ring_y.drain()
    ring_z.drain()


def update(coords, blocks, factor_b, factor_c, factor_a, n_x, n_z):
    half_x, n_grp = n_x // 2, n_x * NC
    vmem = pl.BlockSpec(memory_space=pltpu.VMEM)
    anywhere = pl.BlockSpec(memory_space=pl.ANY)
    dma = pltpu.SemaphoreType.DMA
    rest = BS - ROWS_Z
    f32, bf16 = jnp.float32, jnp.bfloat16
    factor_b, factor_c = factor_b.reshape(-1, BS, R), factor_c.reshape(-1, BS, R)
    jblocks = factor_b.shape[0]
    return pl.pallas_call(
        functools.partial(update_kernel, n_x, n_z),
        out_shape=(
            jax.ShapeDtypeStruct((BS, R), f32),
            jax.ShapeDtypeStruct((R, R), f32),
        ),
        in_specs=[anywhere] * 5,
        out_specs=(vmem, vmem),
        scratch_shapes=[
            pltpu.VMEM(coords.shape, jnp.int32),
            pltpu.SMEM(coords.shape, jnp.int32),
            pltpu.VMEM((BS, R), f32),
            pltpu.SMEM((n_grp,) + coords.shape, jnp.int32),
            pltpu.VMEM(blocks.shape, bf16),
            pltpu.VMEM((NC * jblocks, BS, R), bf16),
            pltpu.VMEM((n_grp - 1, 2, BS, R), bf16),
            pltpu.VMEM((n_x, NC, 2, BS, R), bf16),
            pltpu.VMEM((BS * BS, R), bf16),
            pltpu.VMEM((2 * ROWS_Z + 8, R), f32),
            pltpu.VMEM((2 * rest + 8, R), f32),
            pltpu.VMEM((n_z, NC, 2 * ROWS_Z + 8, R), f32),
            pltpu.VMEM((NY, NC, 2 * rest + 8, R), f32),
            pltpu.VMEM((n_x, NY, ROWS_Z, R), f32),
            pltpu.VMEM((n_x, n_z, rest, R), f32),
            pltpu.VMEM((n_z * NC * 2 + 1, ROWS_Z, R), f32),
            pltpu.VMEM((NY * NC * 2 + 1, rest, R), f32),
            pltpu.VMEM((8, R), jnp.int32),
            pltpu.VMEM((8, R), jnp.int32),
            pltpu.SMEM((8, R), jnp.int32),
            pltpu.SMEM((8, R), jnp.int32),
            pltpu.VMEM((R, R), f32),
            pltpu.VMEM((n_x, R, R), f32),
            pltpu.VMEM((2, R, R), f32),
            pltpu.VMEM((2, R, R), f32),
            pltpu.VMEM((BS, R), f32),
            pltpu.VMEM((8, R), f32),
            pltpu.VMEM((2, half_x, NY, ROWS_Z, R), f32),
            pltpu.VMEM((2, half_x, n_z, rest, R), f32),
            pltpu.VMEM((NY - 1, ROWS_Z, R), f32),
            pltpu.VMEM((n_z - 1, rest, R), f32),
            dma((7,)),
            dma((n_grp - 1,)), dma((n_grp - 1,)),
            dma, dma,
            dma((n_grp - 1,)), dma((n_grp - 1,)),
            dma((n_z - 1,)), dma((n_z - 1,)),
            dma((n_z,)), dma((n_z,)),
            dma((NY - 1,)), dma((NY - 1,)),
            dma((NY,)), dma((NY,)),
            dma((n_x - 1,)), dma((n_x - 1,)),
            dma, dma,
            dma((2, half_x)), dma((2, half_x)),
            dma((2, half_x)), dma((2, half_x)),
            dma((NY - 1,)), dma((NY - 1,)),
            dma((n_z - 1,)), dma((n_z - 1,)),
        ],
        compiler_params=pltpu.CompilerParams(collective_id=0, has_side_effects=True),
        name="update",
    )(coords, blocks, factor_b, factor_c, factor_a)


def sweep_kernel(start_ref, weight_ref, out_ref):
    start, weight = start_ref[...].T, weight_ref[...]
    tiles = [start[8 * k : 8 * k + 8, :] for k in range(R // 8)]
    weights = [weight[8 * k : 8 * k + 8, :] for k in range(R // 8)]
    for r in range(R):
        own, sub = r // 8, r % 8
        fixed = jnp.maximum(jnp.broadcast_to(tiles[own][sub : sub + 1, :], (8, BS)), 0.0)
        for k in range(own, R // 8):
            if k == own and sub == 7:
                continue
            scale = jnp.broadcast_to(weights[k][:, r : r + 1], (8, BS))
            tiles[k] = tiles[k] - scale * fixed
    out_ref[...] = jnp.maximum(jnp.concatenate(tiles, axis=0), 0.0).T


def sweep(start, weight):
    vmem = pl.BlockSpec(memory_space=pltpu.VMEM)
    return pl.pallas_call(
        sweep_kernel,
        out_shape=jax.ShapeDtypeStruct((BS, R), jnp.float32),
        in_specs=[vmem] * 2,
        out_specs=vmem,
        name="sweep",
    )(start, weight)


def body(blocks, coords, factor_a, factor_b, factor_c):
    n_x, n_z = lax.axis_size("grp") // NC, lax.axis_size("rep") // NY
    start, weight = update(coords, blocks, factor_b, factor_c, factor_a, n_x, n_z)
    return sweep(start, weight)


def solution(mesh):
    placed = (
        P(("grp", "rep"), None, None),
        P(("grp", "rep"), None),
        P(("grp", "rep"), None),
        P("grp", None),
        P("grp", None),
    )
    return jax.shard_map(
        body, mesh=mesh, in_specs=placed, out_specs=P(("grp", "rep"), None), check_vma=False
    )
```
